32 devices in a mesh: seg: 4 (over y, x), blk: 8 (over z, core).
Axes of the slice: x: 2, y: 2, z: 4, core: 2. Of those that a mesh axis runs over, the one named last changes fastest.
Arguments:
- state: float32 [32, 4, 16, 2304], P(('seg', 'blk')), may hold values from -6 to 6
- metric: float32 [32, 9, 16, 2304], P(('seg', 'blk')), may hold values from -0.4 to 3, as said below
- block_map: int32 [32], replicated, may hold values from 0 to 31, as said below
- links: int32 [32, 6, 4], replicated, may hold values from -1 to 31, as said below
Outputs:
- advanced: float32 [32, 4, 16, 2304], P(('seg', 'blk'))
The draws below stay inside these ranges and needn't reach their ends.
Inputs may be any that keep to these rules, and one draw needn't show every extreme that they name: A permutation of the block numbers; device slot d = s * 8 + p (segment s, position p along its chain) holds block block_map[d]. `links`: entries are (partner block or -1, partner face, r_i, r_x). Face 0 of the block at position p > 0 joins face 1 of the block at position p - 1 of the same segment, face 1 at p < 7 joins face 0 at p + 1, both with zero flags; faces 0 at p = 0 and 1 at p = 7 have partner -1. A block has at most one of faces 2 to 5 with a partner, and some blocks have one; that partner lies at the same position p in another segment, names this block and face back with the same flags. Unused fields of a face with partner -1 are 0. `metric`: entries 0, 4 and 8 of the second dimension are positive.
All inputs are finite; a program needn't handle non-finite values.
Results may differ from the reference program's by a relative error of at most 0.0003.
Values sent between devices are 32-bit elements; how exact they have to be, the bound alone decides.
A program may use at most 64 MiB of HBM per device.

```python
import math
import jax
import jax.numpy as jnp
from jax import lax

LEN = 16
CROSS = 48
SEGS = 4
CHAIN = 8
BLOCKS = 32


def tree_layout(key):
    base = jax.random.fold_in(key, 101)
    subkeys = jax.random.split(base, 5)
    device_blocks = jax.random.permutation(subkeys[0], BLOCKS).astype(jnp.int32)
    row_keys = jax.random.split(subkeys[1], CHAIN)
    pairings = jax.vmap(lambda row_key: jax.random.permutation(row_key, SEGS))(row_keys).astype(jnp.int32)
    slot_of = jnp.argsort(pairings, axis=1).astype(jnp.int32)
    joined_draw = jax.random.randint(subkeys[2], (CHAIN, SEGS // 2), 0, 2).astype(jnp.int32)
    joined_draw = joined_draw.at[0, 0].set(1)
    face_draw = jax.random.randint(subkeys[3], (CHAIN, SEGS), 2, 6).astype(jnp.int32)
    flip_draw = jax.random.randint(subkeys[4], (CHAIN, SEGS // 2, 2), 0, 2).astype(jnp.int32)
    devices = jnp.arange(BLOCKS, dtype=jnp.int32)
    segment = devices // CHAIN
    position = devices % CHAIN
    slot_index = slot_of[position, segment]
    mate_slot = jnp.bitwise_xor(slot_index, 1)
    pair_index = slot_index // 2
    mate_device = pairings[position, mate_slot] * CHAIN + position
    joined = joined_draw[position, pair_index] == 1
    my_face = face_draw[position, slot_index]
    mate_face = face_draw[position, mate_slot]
    flip_pair = flip_draw[position, pair_index]
    zeros = jnp.zeros((BLOCKS,), jnp.int32)
    has_before = position > 0
    has_after = position < CHAIN - 1
    before = jnp.where(has_before, device_blocks[jnp.clip(devices - 1, 0, BLOCKS - 1)], -1)
    after = jnp.where(has_after, device_blocks[jnp.clip(devices + 1, 0, BLOCKS - 1)], -1)
    rows = [jnp.stack([before, jnp.where(has_before, 1, 0), zeros, zeros], axis=1), jnp.stack([after, zeros, zeros, zeros], axis=1)]
    for side in range(2, 6):
        active = joined & (my_face == side)
        rows.append(jnp.stack([jnp.where(active, device_blocks[mate_device], -1), jnp.where(active, mate_face, 0), jnp.where(active, flip_pair[:, 0], 0), jnp.where(active, flip_pair[:, 1], 0)], axis=1))
    by_device = jnp.stack(rows, axis=1).astype(jnp.int32)
    links = jnp.zeros((BLOCKS, 6, 4), jnp.int32).at[device_blocks].set(by_device)
    return (device_blocks, links)


def draw_block_map(key, part):
    return tree_layout(key)[0]


def draw_links(key, part):
    return tree_layout(key)[1]


def draw_metric(key, part):
    subkeys = jax.random.split(jax.random.fold_in(key, 202), 2)
    dims = (BLOCKS, 9, LEN, CROSS * CROSS)
    diagonal_mask = jnp.array([1, 0, 0, 0, 1, 0, 0, 0, 1], jnp.float32).reshape(1, 9, 1, 1)
    diagonal = jnp.exp(jax.random.uniform(subkeys[0], dims, jnp.float32, math.log(0.5), math.log(2.0)))
    off_diagonal = jax.random.uniform(subkeys[1], dims, jnp.float32, -0.4, 0.4)
    return diagonal_mask * diagonal + (1.0 - diagonal_mask) * off_diagonal


def steps_of(rng, shape, shards, smallest, largest):
    level, own = 1.0, jax.random.fold_in(rng, 6)
    for dim, blocks in shards:
        steps = jnp.exp(jax.random.uniform(jax.random.fold_in(own, dim), (blocks,), jnp.float32, smallest / len(shards), largest / len(shards)))
        level = level * jnp.repeat(steps, shape[dim] // blocks).reshape([-1 if axis == dim else 1 for axis in range(len(shape))])
    return level


def scatter_about(own_key, shape, scale, bound, shards=(), kind=jnp.bfloat16):
    loudness = steps_of(own_key, shape, shards, -0.22, 0.18) if shards else 1.0
    drawn = jax.random.normal(own_key, shape, jnp.float32) * scale * loudness
    return jnp.minimum(jnp.maximum(drawn, -bound), bound).astype(kind)


def setup_inputs(seed: int = 0) -> dict:
    streams_of = jax.random.split(jax.random.key(seed), 5)
    state = scatter_about(streams_of[0], (BLOCKS, 4, LEN, CROSS * CROSS), 1.0, 6.0, ((0, 32),), jnp.float32)
    metric = draw_metric(jax.random.fold_in(streams_of[4], 71), 0)
    block_map = draw_block_map(jax.random.fold_in(streams_of[4], 71), 0)
    links = draw_links(jax.random.fold_in(streams_of[4], 71), 0)
    return dict(state=state, metric=metric, block_map=block_map, links=links)


time_step = 0.05
viscosity = 0.2
compress = 1.0


def wall_mirror():
    return jnp.array([-1.0, -1.0, -1.0, 1.0], jnp.float32).reshape(4, 1, 1)


def shifted(extended, direction, offset):
    count = extended.shape[direction] - 4
    return lax.slice_in_dim(extended, offset, offset + count, axis=direction)


def slope(extended, direction):
    return (shifted(extended, direction, 0) - 8.0 * shifted(extended, direction, 1)
            + 8.0 * shifted(extended, direction, 3) - shifted(extended, direction, 4)) / 12.0


def curvature(extended, direction):
    return (-shifted(extended, direction, 0) + 16.0 * shifted(extended, direction, 1)
            - 30.0 * shifted(extended, direction, 2) + 16.0 * shifted(extended, direction, 3)
            - shifted(extended, direction, 4)) / 12.0


def rates(block_state, geometry, padded):
    slopes = [slope(padded[direction], direction + 1) for direction in range(3)]
    bends = [curvature(padded[direction], direction + 1) for direction in range(3)]
    contravariant = []
    metric_norms = []
    for direction in range(3):
        base = 3 * direction
        contravariant.append(geometry[base] * block_state[0] + geometry[base + 1] * block_state[1]
                             + geometry[base + 2] * block_state[2])
        metric_norms.append(geometry[base] * geometry[base] + geometry[base + 1] * geometry[base + 1]
                            + geometry[base + 2] * geometry[base + 2])
    results = []
    for component in range(3):
        convect = sum(contravariant[direction] * slopes[direction][component] for direction in range(3))
        gradient = sum(geometry[3 * direction + component] * slopes[direction][3] for direction in range(3))
        diffuse = sum(metric_norms[direction] * bends[direction][component] for direction in range(3))
        results.append(-convect - gradient + viscosity * diffuse)
    divergence = sum(geometry[3 * direction + component] * slopes[direction][component]
                     for direction in range(3) for component in range(3))
    results.append(-compress * divergence)
    return jnp.stack(results)


def lateral_faces(block_state):
    edge = block_state.shape[2]
    lower_j = jnp.stack([block_state[:, :, 0, :], block_state[:, :, 1, :]])
    upper_j = jnp.stack([block_state[:, :, edge - 1, :], block_state[:, :, edge - 2, :]])
    lower_k = jnp.stack([block_state[:, :, :, 0], block_state[:, :, :, 1]])
    upper_k = jnp.stack([block_state[:, :, :, edge - 1], block_state[:, :, :, edge - 2]])
    return jnp.stack([lower_j, upper_j, lower_k, upper_k])


def pad_lateral(block_state, ghost_layers):
    lower_j = jnp.stack([ghost_layers[0][1], ghost_layers[0][0]], axis=2)
    upper_j = jnp.stack([ghost_layers[1][0], ghost_layers[1][1]], axis=2)
    lower_k = jnp.stack([ghost_layers[2][1], ghost_layers[2][0]], axis=3)
    upper_k = jnp.stack([ghost_layers[3][0], ghost_layers[3][1]], axis=3)
    across_first = jnp.concatenate([lower_j, block_state, upper_j], axis=2)
    across_second = jnp.concatenate([lower_k, block_state, upper_k], axis=3)
    return across_first, across_second


def orient(layers, flip_along, flip_across):
    layers = jnp.where(flip_along == 1, jnp.flip(layers, 2), layers)
    return jnp.where(flip_across == 1, jnp.flip(layers, 3), layers)


def open_rows(block_state):
    mirror = -wall_mirror()
    lower = jnp.stack([mirror * block_state[:, 1], mirror * block_state[:, 0]], axis=1)
    upper = jnp.stack([mirror * block_state[:, -1], mirror * block_state[:, -2]], axis=1)
    return lower, upper


def device_of(block_map, block):
    return jnp.argmax(block_map == jnp.maximum(block, 0)).astype(jnp.int32)


def reference(state, metric, block_map, links):
    count = state.shape[0]
    length = state.shape[2]
    whole = state.reshape(count, 4, length, CROSS, CROSS)
    geometry_all = metric.reshape(count, 9, length, CROSS, CROSS)

    def all_rates(current):
        face_layers = jax.vmap(lateral_faces)(current)

        def per_block(device):
            block_state = current[device]
            entries = links[block_map[device]]
            open_lower, open_upper = open_rows(block_state)
            before = current[device_of(block_map, entries[0, 0])][:, length - 2:]
            after = current[device_of(block_map, entries[1, 0])][:, :2]
            lower = jnp.where(entries[0, 0] >= 0, before, open_lower)
            upper = jnp.where(entries[1, 0] >= 0, after, open_upper)
            along_vessel = jnp.concatenate([lower, block_state, upper], axis=1)
            ghost_layers = []
            for side in range(4):
                entry = entries[2 + side]
                partner = face_layers[device_of(block_map, entry[0]), jnp.clip(entry[1] - 2, 0, 3)]
                partner = orient(partner, entry[2], entry[3])
                ghost_layers.append(jnp.where(entry[0] >= 0, partner, wall_mirror() * face_layers[device, side]))
            across_first, across_second = pad_lateral(block_state, ghost_layers)
            return rates(block_state, geometry_all[device], (along_vessel, across_first, across_second))

        return lax.map(per_block, jnp.arange(count, dtype=jnp.int32))

    first_section = whole + time_step * all_rates(whole)
    advanced = 0.5 * whole + 0.5 * (first_section + time_step * all_rates(first_section))
    return advanced.reshape(state.shape)
```

```python
import functools
import math

import jax
import jax.numpy as jnp
from jax import lax
from jax.experimental import pallas as pl
from jax.experimental.pallas import tpu as pltpu
from jax.sharding import PartitionSpec as P

time_step = 0.05
viscosity = 0.2
compress = 1.0
MESH = pl.DeviceIdType.MESH
LANES = 128
WALL = (-1.0, -1.0, -1.0, 1.0)


def split_index(index, size, count):
    quotient = jnp.zeros_like(index)
    for step in range(1, count):
        quotient += (index >= size * step).astype(jnp.int32)
    return quotient, index - size * quotient


def halves(value):
    lead = value.astype(jnp.bfloat16)
    return lead, (value - lead.astype(jnp.float32)).astype(jnp.bfloat16)


def select(flag, yes, no):
    return jnp.where(flag, yes, no)


def kernel(segs, chain, cross, state_hbm, metric_hbm, block_map, links, out_ref,
           first, second, geometry, total, pack_matrix, slope_matrix, bend_matrix,
           low_out, high_out, low_in, high_in, face_out, face_in,
           load_sem, chain_send, chain_recv, face_send, face_recv):
    length, width = out_ref.shape[1], out_ref.shape[2]
    chunk = math.lcm(cross, LANES)
    chunks = width // chunk
    inner = pl.ds(LANES, width)
    seg, pos = lax.axis_index("seg"), lax.axis_index("blk")
    me = seg * chain + pos
    has_before, has_after = pos > 0, pos < chain - 1
    before, after = lax.rem(pos + chain - 1, chain), lax.rem(pos + 1, chain)

    load_state = pltpu.make_async_copy(state_hbm.at[0], first.at[:, :, inner], load_sem.at[0])
    load_metric = pltpu.make_async_copy(metric_hbm.at[0], geometry, load_sem.at[1])
    load_state.start()
    load_metric.start()

    barrier = pltpu.get_barrier_semaphore()
    for offset in range(1, segs):
        pl.semaphore_signal(barrier, inc=1, device_id={"seg": lax.rem(seg + offset, segs)}, device_id_type=MESH)

    @pl.when(has_before)
    def _():
        pl.semaphore_signal(barrier, inc=1, device_id={"blk": before}, device_id_type=MESH)

    @pl.when(has_after)
    def _():
        pl.semaphore_signal(barrier, inc=1, device_id={"blk": after}, device_id_type=MESH)

    block = block_map[me]
    joins = [links[2 + side, 0, block] >= 0 for side in range(4)]
    partner, flip_along, flip_across = jnp.int32(-1), jnp.int32(0), jnp.int32(0)
    for side in range(4):
        partner = select(joins[side], links[2 + side, 0, block], partner)
        flip_along = select(joins[side], links[2 + side, 2, block], flip_along)
        flip_across = select(joins[side], links[2 + side, 3, block], flip_across)
    any_join = partner >= 0
    on_first = jnp.logical_or(joins[0], joins[1])
    on_high = jnp.logical_or(joins[1], joins[3])
    own_layers = [select(join, 0.0, 1.0) for join in joins]
    layer_stride = select(on_first, cross, 1)
    cell_stride = select(on_first, 1, cross)
    comes_from = []
    for offset in range(1, segs):
        device = lax.rem(seg + segs - offset, segs) * chain + pos
        comes_from.append(jnp.logical_and(any_join, block_map[device] == partner))

    pads = jnp.zeros((4, length, LANES), jnp.float32)
    for padded in (first, second):
        padded[:, :, :LANES] = pads
        padded[:, :, LANES + width:] = pads

    column = lax.broadcasted_iota(jnp.int32, (1, LANES), 1)
    layer, place = split_index(column, cross, 3)
    layer_place = select(on_high, cross - 1 - layer, layer)
    source = layer_place * layer_stride + place * cell_stride
    source = jnp.where(jnp.logical_and(layer < 2, any_join), source, -1)
    piece = 2 * LANES
    for part in range(width // piece):
        cells = lax.broadcasted_iota(jnp.int32, (piece, LANES), 0) + part * piece
        pack_matrix[part * piece:(part + 1) * piece, :] = (cells == source).astype(jnp.float32).astype(jnp.bfloat16)

    def pack(padded, turn):
        for c in range(4):
            for layer_index in range(2):
                row = 2 * c + layer_index
                low_out[turn, row:row + 1, :] = padded[c, layer_index:layer_index + 1, inner]
                high_out[turn, row:row + 1, :] = padded[c, length - 1 - layer_index:length - layer_index, inner]

    def pack_face(padded, turn):
        rows = 4 * length
        packed = jnp.zeros((2 * rows, LANES), jnp.float32)
        for part in range(width // piece):
            value = padded[:, :, LANES + part * piece:LANES + (part + 1) * piece].reshape(rows, piece)
            both = jnp.concatenate(halves(value), axis=0)
            packed += jnp.dot(both, pack_matrix[part * piece:(part + 1) * piece, :], preferred_element_type=jnp.float32)
        face_out[turn] = packed[:rows] + packed[rows:]

    def chain_copies(turn):
        to_before = pltpu.make_async_remote_copy(
            low_out.at[turn], high_in.at[turn], chain_send.at[turn, 0], chain_recv.at[turn, 0],
            device_id={"blk": before}, device_id_type=MESH)
        to_after = pltpu.make_async_remote_copy(
            high_out.at[turn], low_in.at[turn], chain_send.at[turn, 1], chain_recv.at[turn, 1],
            device_id={"blk": after}, device_id_type=MESH)
        return to_before, to_after

    def face_copies(turn):
        return [pltpu.make_async_remote_copy(
            face_out.at[turn], face_in.at[turn, offset - 1], face_send.at[turn, offset - 1],
            face_recv.at[turn, offset - 1], device_id={"seg": lax.rem(seg + offset, segs)}, device_id_type=MESH)
            for offset in range(1, segs)]

    def start_chain(turn):
        to_before, to_after = chain_copies(turn)

        @pl.when(has_before)
        def _():
            to_before.start()

        @pl.when(has_after)
        def _():
            to_after.start()

    def start_faces(turn):
        for copy in face_copies(turn):
            copy.start()

    def await_all(turn):
        to_before, to_after = chain_copies(turn)

        @pl.when(has_before)
        def _():
            to_before.wait_send()
            to_after.wait_recv()

        @pl.when(has_after)
        def _():
            to_after.wait_send()
            to_before.wait_recv()

        for copy in face_copies(turn):
            copy.wait()

    def build_spread():
        row = lax.broadcasted_iota(jnp.int32, (LANES, 1), 0)
        layer, place = split_index(row, cross, 3)
        place = select(flip_across == 1, cross - 1 - place, place)
        valid = jnp.logical_and(layer < 2, any_join)
        near = select(on_high, cross - 1, 0)
        spot = select(on_high, cross - 2 + layer, 1 - layer)
        outer = jnp.where(valid, spot * layer_stride + place * cell_stride, -1)
        edge = jnp.where(jnp.logical_and(valid, layer == 0), near * layer_stride + place * cell_stride, -1)
        sign = select(on_high, -1.0, 1.0)
        for part in range(width // LANES):
            cells = lax.broadcasted_iota(jnp.int32, (LANES, LANES), 1) + part * LANES
            is_outer = (cells == outer).astype(jnp.float32)
            is_edge = (cells == edge).astype(jnp.float32)
            slope = (sign * (is_outer - 8.0 * is_edge)).astype(jnp.bfloat16)
            bend = (16.0 * is_edge - is_outer).astype(jnp.bfloat16)
            at = slice(part * LANES, (part + 1) * LANES)
            slope_matrix[:LANES, at] = slope
            slope_matrix[LANES:, at] = slope
            bend_matrix[:LANES, at] = bend
            bend_matrix[LANES:, at] = bend

    lane = lax.broadcasted_iota(jnp.int32, (length, chunk), 1)
    row_of = lax.broadcasted_iota(jnp.int32, (length, chunk), 0)
    _, lane_k = split_index(lane, cross, chunk // cross)

    def central(value, minus2, minus1, plus1, plus2, bent):
        slope = (minus2 - plus2) + 8.0 * (plus1 - minus1)
        if not bent:
            return slope, None
        return slope, 16.0 * (minus1 + plus1) - (minus2 + plus2) - 30.0 * value

    def along(value, bent):
        def moved(step):
            rolled = pltpu.roll(value, step % length, 0)
            inside = row_of >= step if step > 0 else row_of < length + step
            return jnp.where(inside, rolled, 0.0)
        return central(value, moved(2), moved(1), moved(-1), moved(-2), bent)

    def across(wide, value, stride, index, low_factor, high_factor, bent):
        def moved(step):
            if step > 0:
                return pltpu.roll(wide[:, :LANES + chunk], step, 1)[:, LANES:]
            span = LANES + chunk
            return pltpu.roll(wide[:, LANES:], span + step, 1)[:, :chunk]
        minus2, minus1, plus1, plus2 = moved(2 * stride), moved(stride), moved(-stride), moved(-2 * stride)
        at0, at1, at_last1, at_last = index
        m1 = jnp.where(at0, low_factor * value, minus1)
        p1 = jnp.where(at_last, high_factor * value, plus1)
        m2 = jnp.where(at0, low_factor * plus1, jnp.where(at1, low_factor * minus1, minus2))
        p2 = jnp.where(at_last, high_factor * minus1, jnp.where(at_last1, high_factor * plus1, plus2))
        return central(value, m2, m1, p1, p2, bent)

    def weights(metric, values):
        carried = metric[0] * values[0] + metric[1] * values[1] + metric[2] * values[2]
        norm = viscosity * (metric[0] * metric[0] + metric[1] * metric[1] + metric[2] * metric[2])
        return carried, norm

    def rates_of(metric, values, slopes, bends):
        carried, norm = weights(metric, values)
        parts = [norm * bends[c] - carried * slopes[c] - metric[c] * slopes[3] for c in range(3)]
        parts.append(-compress * (metric[0] * slopes[0] + metric[1] * slopes[1] + metric[2] * slopes[2]))
        return parts

    def inside_rates(padded):
        def body(step, carry):
            start = pl.multiple_of(step * chunk, LANES)
            cell = lane + step * chunk
            k_at = (lane_k == 0, lane_k == 1, lane_k == cross - 2, lane_k == cross - 1)
            j_at = (cell < cross, jnp.logical_and(cell >= cross, cell < 2 * cross),
                    jnp.logical_and(cell >= width - 2 * cross, cell < width - cross), cell >= width - cross)
            wide = [padded[c, :, pl.ds(start, chunk + 2 * LANES)] for c in range(4)]
            values = [w[:, LANES:LANES + chunk] for w in wide]
            sums = None
            for direction in range(3):
                metric = [geometry[3 * direction + b, :, pl.ds(start, chunk)] for b in range(3)]
                slopes, bends = [], []
                for c in range(4):
                    if direction == 0:
                        slope, bend = along(values[c], c < 3)
                    else:
                        stride, at = ((cross, j_at), (1, k_at))[direction - 1]
                        low = WALL[c] * own_layers[2 * direction - 2]
                        high = WALL[c] * own_layers[2 * direction - 1]
                        slope, bend = across(wide[c], values[c], stride, at, low, high, c < 3)
                    slopes.append(slope)
                    bends.append(bend)
                parts = rates_of(metric, values, slopes, bends)
                sums = parts if sums is None else [a + b for a, b in zip(sums, parts)]
            for c in range(4):
                total[c, :, pl.ds(start, chunk)] = sums[c]
            return carry

        lax.fori_loop(0, chunks, body, 0)

    def outside_rates(padded, turn, finish):
        received = jnp.zeros((4 * length, LANES), jnp.float32)
        for index, here in enumerate(comes_from):
            received = jnp.where(here, face_in[turn, index], received)
        both = jnp.concatenate(halves(received), axis=1)
        target = lax.broadcasted_iota(jnp.int32, (4 * length, 1), 0)
        component, along_index = split_index(target, length, 4)
        along_index = select(flip_along == 1, length - 1 - along_index, along_index)
        target = component * length + along_index
        swap = (lax.broadcasted_iota(jnp.int32, (4 * length, 4 * length), 1) == target)
        swap = swap.astype(jnp.float32).astype(jnp.bfloat16)
        both = jnp.dot(swap, both, preferred_element_type=jnp.float32).astype(jnp.bfloat16)

        def body(step, carry):
            start = pl.multiple_of(step * chunk, LANES)
            at = pl.ds(start, chunk)
            values = [padded[c, :, pl.ds(pl.multiple_of(start + LANES, LANES), chunk)] for c in range(4)]
            metric = [geometry[b, :, at] for b in range(3)]
            low_own, high_own = low_out[turn, :, at], high_out[turn, :, at]
            low_got, high_got = low_in[turn, :, at], high_in[turn, :, at]
            slopes, bends = [], []
            for c in range(4):
                ghosts = []
                for got, own, there in ((low_got, low_own, has_before), (high_got, high_own, has_after)):
                    for layer_index in range(2):
                        row = 2 * c + layer_index
                        ghosts.append(jnp.where(there, got[row:row + 1], -WALL[c] * own[row:row + 1]))
                low0, low1, high0, high1 = ghosts
                slope = jnp.where(row_of == 0, low1 - 8.0 * low0, 0.0)
                slope = jnp.where(row_of == 1, low0, slope)
                slope = jnp.where(row_of == length - 2, -high0, slope)
                slopes.append(jnp.where(row_of == length - 1, 8.0 * high0 - high1, slope))
                if c < 3:
                    bend = jnp.where(row_of == 0, 16.0 * low0 - low1, 0.0)
                    bend = jnp.where(row_of == 1, -low0, bend)
                    bend = jnp.where(row_of == length - 2, -high0, bend)
                    bends.append(jnp.where(row_of == length - 1, 16.0 * high0 - high1, bend))
            sums = rates_of(metric, values, slopes, bends)
            metric = [jnp.where(on_first, geometry[3 + b, :, at], geometry[6 + b, :, at]) for b in range(3)]
            slope = jnp.dot(both, slope_matrix[:, at], preferred_element_type=jnp.float32)
            bend = jnp.dot(both[:3 * length], bend_matrix[:, at], preferred_element_type=jnp.float32)
            slopes = [slope[c * length:(c + 1) * length] for c in range(4)]
            bends = [bend[c * length:(c + 1) * length] for c in range(3)]
            parts = rates_of(metric, values, slopes, bends)
            for c in range(4):
                finish(c, start, values[c], total[c, :, at] + sums[c] + parts[c])
            return carry

        lax.fori_loop(0, chunks, body, 0)

    def finish_first(c, start, value, rate):
        second[c, :, pl.ds(pl.multiple_of(start + LANES, LANES), chunk)] = value + (time_step / 12.0) * rate

    def finish_second(c, start, value, rate):
        base = first[c, :, pl.ds(pl.multiple_of(start + LANES, LANES), chunk)]
        out_ref[c, :, pl.ds(start, chunk)] = 0.5 * base + 0.5 * (value + (time_step / 12.0) * rate)

    load_state.wait()
    pack(first, 0)
    pl.semaphore_wait(barrier, segs - 1 + has_before.astype(jnp.int32) + has_after.astype(jnp.int32))

    start_chain(0)
    pack_face(first, 0)
    start_faces(0)
    build_spread()
    load_metric.wait()
    inside_rates(first)
    await_all(0)
    outside_rates(first, 0, finish_first)

    pack(second, 1)
    start_chain(1)
    pack_face(second, 1)
    start_faces(1)
    inside_rates(second)
    await_all(1)
    outside_rates(second, 1, finish_second)


def on_device(state, metric, block_map, links):
    segs, chain = lax.axis_size("seg"), lax.axis_size("blk")
    _, parts, length, width = state.shape
    cross = math.isqrt(width)
    f32, bf16, dma = jnp.float32, jnp.bfloat16, pltpu.SemaphoreType.DMA
    result = pl.pallas_call(
        functools.partial(kernel, segs, chain, cross),
        out_shape=jax.ShapeDtypeStruct((parts, length, width), f32),
        in_specs=[pl.BlockSpec(memory_space=pl.ANY)] * 2 + [pl.BlockSpec(memory_space=pltpu.SMEM)] * 2,
        out_specs=pl.BlockSpec(memory_space=pltpu.VMEM),
        scratch_shapes=[
            pltpu.VMEM((parts, length, width + 2 * LANES), f32),
            pltpu.VMEM((parts, length, width + 2 * LANES), f32),
            pltpu.VMEM((9, length, width), f32),
            pltpu.VMEM((parts, length, width), f32),
            pltpu.VMEM((width, LANES), bf16),
            pltpu.VMEM((2 * LANES, width), bf16),
            pltpu.VMEM((2 * LANES, width), bf16),
            pltpu.VMEM((2, 2 * parts, width), f32),
            pltpu.VMEM((2, 2 * parts, width), f32),
            pltpu.VMEM((2, 2 * parts, width), f32),
            pltpu.VMEM((2, 2 * parts, width), f32),
            pltpu.VMEM((2, parts * length, LANES), f32),
            pltpu.VMEM((2, segs - 1, parts * length, LANES), f32),
            dma((2,)), dma((2, 2)), dma((2, 2)), dma((2, segs - 1)), dma((2, segs - 1)),
        ],
        compiler_params=pltpu.CompilerParams(collective_id=0, has_side_effects=True),
    )(state, metric, block_map, links.transpose(1, 2, 0))
    return result.reshape(state.shape)


def solution(mesh):
    in_specs = (P(("seg", "blk"), None, None, None), P(("seg", "blk"), None, None, None), P(), P())
    out_specs = P(("seg", "blk"), None, None, None)
    return jax.shard_map(
        on_device, mesh=mesh, in_specs=in_specs, out_specs=out_specs, check_vma=False
    )
```

```python
import functools
import math

import jax
import jax.numpy as jnp
from jax import lax
from jax.experimental import pallas as pl
from jax.experimental.pallas import tpu as pltpu
from jax.sharding import PartitionSpec as P

time_step = 0.05
viscosity = 0.2
compress = 1.0
MESH = pl.DeviceIdType.MESH
LANES = 128
WALL = (-1.0, -1.0, -1.0, 1.0)


def split_index(index, size, count):
    quotient = jnp.zeros_like(index)
    for step in range(1, count):
        quotient += (index >= size * step).astype(jnp.int32)
    return quotient, index - size * quotient


def halves(value):
    lead = value.astype(jnp.bfloat16)
    return lead, (value - lead.astype(jnp.float32)).astype(jnp.bfloat16)


def select(flag, yes, no):
    return jnp.where(flag, yes, no)


def kernel(segs, chain, cross, state_hbm, metric_hbm, block_map, links, out_ref,
           first, second, geometry, total, pack_matrix, slope_matrix, bend_matrix,
           split, k_slope_uvw, k_slope_p, k_bend, slope_k, bend_k,
           low_out, high_out, low_in, high_in, face_out, face_in,
           load_sem, chain_send, chain_recv, face_send, face_recv):
    length, width = out_ref.shape[1], out_ref.shape[2]
    chunk = math.lcm(cross, LANES)
    chunks = width // chunk
    inner = pl.ds(LANES, width)
    seg, pos = lax.axis_index("seg"), lax.axis_index("blk")
    me = seg * chain + pos
    has_before, has_after = pos > 0, pos < chain - 1
    before, after = lax.rem(pos + chain - 1, chain), lax.rem(pos + 1, chain)

    load_state = pltpu.make_async_copy(state_hbm.at[0], first.at[:, :, inner], load_sem.at[0])
    load_metric = pltpu.make_async_copy(metric_hbm.at[0], geometry, load_sem.at[1])
    load_state.start()
    load_metric.start()

    barrier = pltpu.get_barrier_semaphore()
    for offset in range(1, segs):
        pl.semaphore_signal(barrier, inc=1, device_id={"seg": lax.rem(seg + offset, segs)}, device_id_type=MESH)

    @pl.when(has_before)
    def _():
        pl.semaphore_signal(barrier, inc=1, device_id={"blk": before}, device_id_type=MESH)

    @pl.when(has_after)
    def _():
        pl.semaphore_signal(barrier, inc=1, device_id={"blk": after}, device_id_type=MESH)

    block = block_map[me]
    joins = [links[2 + side, 0, block] >= 0 for side in range(4)]
    partner, flip_along, flip_across = jnp.int32(-1), jnp.int32(0), jnp.int32(0)
    for side in range(4):
        partner = select(joins[side], links[2 + side, 0, block], partner)
        flip_along = select(joins[side], links[2 + side, 2, block], flip_along)
        flip_across = select(joins[side], links[2 + side, 3, block], flip_across)
    any_join = partner >= 0
    on_first = jnp.logical_or(joins[0], joins[1])
    on_high = jnp.logical_or(joins[1], joins[3])
    own_layers = [select(join, 0.0, 1.0) for join in joins]
    layer_stride = select(on_first, cross, 1)
    cell_stride = select(on_first, 1, cross)
    comes_from = []
    for offset in range(1, segs):
        device = lax.rem(seg + segs - offset, segs) * chain + pos
        comes_from.append(jnp.logical_and(any_join, block_map[device] == partner))

    pads = jnp.zeros((4, length, LANES), jnp.float32)
    for padded in (first, second):
        padded[:, :, :LANES] = pads
        padded[:, :, LANES + width:] = pads

    column = lax.broadcasted_iota(jnp.int32, (1, LANES), 1)
    layer, place = split_index(column, cross, 3)
    layer_place = select(on_high, cross - 1 - layer, layer)
    source = layer_place * layer_stride + place * cell_stride
    source = jnp.where(jnp.logical_and(layer < 2, any_join), source, -1)
    piece = 2 * LANES
    for part in range(width // piece):
        cells = lax.broadcasted_iota(jnp.int32, (piece, LANES), 0) + part * piece
        pack_matrix[part * piece:(part + 1) * piece, :] = (cells == source).astype(jnp.float32).astype(jnp.bfloat16)

    def pack(padded, turn):
        for c in range(4):
            for layer_index in range(2):
                row = 2 * c + layer_index
                low_out[turn, row:row + 1, :] = padded[c, layer_index:layer_index + 1, inner]
                high_out[turn, row:row + 1, :] = padded[c, length - 1 - layer_index:length - layer_index, inner]

    def pack_face(padded, turn):
        rows = 4 * length
        lead, trail = halves(padded[:, :, inner].reshape(rows, width))
        split[0] = lead
        split[1] = trail
        both = jnp.concatenate([lead, trail], axis=0)
        packed = jnp.dot(both, pack_matrix[...], preferred_element_type=jnp.float32)
        face_out[turn] = packed[:rows] + packed[rows:]

    def build_k():
        for matrix in (k_slope_uvw, k_slope_p, k_bend):
            matrix[...] = jnp.zeros((2 * chunk, chunk), jnp.bfloat16)
        low, high = own_layers[2], own_layers[3]
        here = lax.broadcasted_iota(jnp.int32, (cross, LANES), 0)
        column = lax.broadcasted_iota(jnp.int32, (cross, LANES), 1)
        for group in range(chunk // cross):
            first_row = group * cross
            for tile in range(first_row // LANES, (first_row + cross - 1) // LANES + 1):
                there = column + (tile * LANES - first_row)
                there = jnp.where(jnp.logical_and(there >= 0, there < cross), there, 4 * width)
                offset, mirrored = here - there, here + there

                def at(index, value, factor):
                    return jnp.where(index == value, factor, 0.0)

                slope = at(offset, -2, 1.0) + at(offset, -1, -8.0) + at(offset, 1, 8.0) + at(offset, 2, -1.0)
                bend = (at(offset, -2, -1.0) + at(offset, -1, 16.0) + at(offset, 0, -30.0)
                        + at(offset, 1, 16.0) + at(offset, 2, -1.0))
                end = 2 * cross - 2
                wall_slope = (at(mirrored, 0, -8.0 * low) + at(mirrored, 1, low)
                              + at(mirrored, end, 8.0 * high) + at(mirrored, end - 1, -high))
                wall_bend = (at(mirrored, 0, 16.0 * low) + at(mirrored, 1, -low)
                             + at(mirrored, end, 16.0 * high) + at(mirrored, end - 1, -high))
                lanes = slice(tile * LANES, (tile + 1) * LANES)
                for matrix, value in ((k_slope_uvw, slope + WALL[0] * wall_slope),
                                      (k_slope_p, slope + WALL[3] * wall_slope),
                                      (k_bend, bend + WALL[0] * wall_bend)):
                    value = value.astype(jnp.bfloat16)
                    matrix[first_row:first_row + cross, lanes] = value
                    matrix[chunk + first_row:chunk + first_row + cross, lanes] = value

    def along_k():
        rows = 3 * length
        parts = []
        for step in range(chunks):
            at = slice(step * chunk, (step + 1) * chunk)
            parts.append(jnp.concatenate([split[0, :, at], split[1, :, at]], axis=1))
        velocity = jnp.concatenate([part[:rows] for part in parts], axis=0)
        pressure = jnp.concatenate([part[rows:] for part in parts], axis=0)
        slope = jnp.dot(velocity, k_slope_uvw[...], preferred_element_type=jnp.float32)
        bend = jnp.dot(velocity, k_bend[...], preferred_element_type=jnp.float32)
        slope_p = jnp.dot(pressure, k_slope_p[...], preferred_element_type=jnp.float32)
        for step in range(chunks):
            at = slice(step * chunk, (step + 1) * chunk)
            slope_k[:3, :, at] = slope[step * rows:(step + 1) * rows].reshape(3, length, chunk)
            bend_k[:, :, at] = bend[step * rows:(step + 1) * rows].reshape(3, length, chunk)
            slope_k[3, :, at] = slope_p[step * length:(step + 1) * length]

    def chain_copies(turn):
        to_before = pltpu.make_async_remote_copy(
            low_out.at[turn], high_in.at[turn], chain_send.at[turn, 0], chain_recv.at[turn, 0],
            device_id={"blk": before}, device_id_type=MESH)
        to_after = pltpu.make_async_remote_copy(
            high_out.at[turn], low_in.at[turn], chain_send.at[turn, 1], chain_recv.at[turn, 1],
            device_id={"blk": after}, device_id_type=MESH)
        return to_before, to_after

    def face_copies(turn):
        return [pltpu.make_async_remote_copy(
            face_out.at[turn], face_in.at[turn, offset - 1], face_send.at[turn, offset - 1],
            face_recv.at[turn, offset - 1], device_id={"seg": lax.rem(seg + offset, segs)}, device_id_type=MESH)
            for offset in range(1, segs)]

    def start_chain(turn):
        to_before, to_after = chain_copies(turn)

        @pl.when(has_before)
        def _():
            to_before.start()

        @pl.when(has_after)
        def _():
            to_after.start()

    def start_faces(turn):
        for copy in face_copies(turn):
            copy.start()

    def await_all(turn):
        to_before, to_after = chain_copies(turn)

        @pl.when(has_before)
        def _():
            to_before.wait_send()
            to_after.wait_recv()

        @pl.when(has_after)
        def _():
            to_after.wait_send()
            to_before.wait_recv()

        for copy in face_copies(turn):
            copy.wait()

    def build_spread():
        row = lax.broadcasted_iota(jnp.int32, (LANES, 1), 0)
        layer, place = split_index(row, cross, 3)
        place = select(flip_across == 1, cross - 1 - place, place)
        valid = jnp.logical_and(layer < 2, any_join)
        near = select(on_high, cross - 1, 0)
        spot = select(on_high, cross - 2 + layer, 1 - layer)
        outer = jnp.where(valid, spot * layer_stride + place * cell_stride, -1)
        edge = jnp.where(jnp.logical_and(valid, layer == 0), near * layer_stride + place * cell_stride, -1)
        sign = select(on_high, -1.0, 1.0)
        for part in range(width // LANES):
            cells = lax.broadcasted_iota(jnp.int32, (LANES, LANES), 1) + part * LANES
            is_outer = (cells == outer).astype(jnp.float32)
            is_edge = (cells == edge).astype(jnp.float32)
            slope = (sign * (is_outer - 8.0 * is_edge)).astype(jnp.bfloat16)
            bend = (16.0 * is_edge - is_outer).astype(jnp.bfloat16)
            at = slice(part * LANES, (part + 1) * LANES)
            slope_matrix[:LANES, at] = slope
            slope_matrix[LANES:, at] = slope
            bend_matrix[:LANES, at] = bend
            bend_matrix[LANES:, at] = bend

    lane = lax.broadcasted_iota(jnp.int32, (length, chunk), 1)
    row_of = lax.broadcasted_iota(jnp.int32, (length, chunk), 0)

    def central(value, minus2, minus1, plus1, plus2, bent):
        slope = (minus2 - plus2) + 8.0 * (plus1 - minus1)
        if not bent:
            return slope, None
        return slope, 16.0 * (minus1 + plus1) - (minus2 + plus2) - 30.0 * value

    def along(value, bent):
        def moved(step):
            rolled = pltpu.roll(value, step % length, 0)
            inside = row_of >= step if step > 0 else row_of < length + step
            return jnp.where(inside, rolled, 0.0)
        return central(value, moved(2), moved(1), moved(-1), moved(-2), bent)

    def along_j(wide, value, low_factor, high_factor, bent):
        def moved(step):
            if step > 0:
                return pltpu.roll(wide[:, :LANES + chunk], step, 1)[:, LANES:]
            return pltpu.roll(wide[:, LANES:], LANES + chunk + step, 1)[:, :chunk]
        minus2, minus1, plus1, plus2 = moved(2 * cross), moved(cross), moved(-cross), moved(-2 * cross)
        m1, m2, p1, p2 = minus1, minus2, plus1, plus2
        if low_factor is not None:
            m1 = jnp.where(lane < cross, low_factor * value, minus1)
            m2 = jnp.where(lane < cross, low_factor * plus1, jnp.where(lane < 2 * cross, low_factor * minus1, minus2))
        if high_factor is not None:
            p1 = jnp.where(lane >= chunk - cross, high_factor * value, plus1)
            p2 = jnp.where(lane >= chunk - cross, high_factor * minus1,
                           jnp.where(lane >= chunk - 2 * cross, high_factor * plus1, plus2))
        return central(value, m2, m1, p1, p2, bent)

    def weights(metric, values):
        carried = metric[0] * values[0] + metric[1] * values[1] + metric[2] * values[2]
        norm = viscosity * (metric[0] * metric[0] + metric[1] * metric[1] + metric[2] * metric[2])
        return carried, norm

    def rates_of(metric, values, slopes, bends):
        carried, norm = weights(metric, values)
        parts = [norm * bends[c] - carried * slopes[c] - metric[c] * slopes[3] for c in range(3)]
        parts.append(-compress * (metric[0] * slopes[0] + metric[1] * slopes[1] + metric[2] * slopes[2]))
        return parts

    def inside_rates(padded):
        def at_chunk(start, is_first, is_last):
            at = pl.ds(start, chunk)
            wide = [padded[c, :, pl.ds(start, chunk + 2 * LANES)] for c in range(4)]
            values = [w[:, LANES:LANES + chunk] for w in wide]
            sums = None
            for direction in range(3):
                metric = [geometry[3 * direction + b, :, at] for b in range(3)]
                if direction == 2:
                    slopes = [slope_k[c, :, at] for c in range(4)]
                    bends = [bend_k[c, :, at] for c in range(3)]
                else:
                    slopes, bends = [], []
                    for c in range(4):
                        if direction == 0:
                            slope, bend = along(values[c], c < 3)
                        else:
                            low = WALL[c] * own_layers[0] if is_first else None
                            high = WALL[c] * own_layers[1] if is_last else None
                            slope, bend = along_j(wide[c], values[c], low, high, c < 3)
                        slopes.append(slope)
                        bends.append(bend)
                parts = rates_of(metric, values, slopes, bends)
                sums = parts if sums is None else [a + b for a, b in zip(sums, parts)]
            for c in range(4):
                total[c, :, at] = sums[c]

        at_chunk(0, True, chunks == 1)
        if chunks > 2:
            @pl.loop(1, chunks - 1)
            def _(step):
                at_chunk(pl.multiple_of(step * chunk, LANES), False, False)
        if chunks > 1:
            at_chunk((chunks - 1) * chunk, False, True)

    def outside_rates(padded, turn, finish):
        received = jnp.zeros((4 * length, LANES), jnp.float32)
        for index, here in enumerate(comes_from):
            received = jnp.where(here, face_in[turn, index], received)
        both = jnp.concatenate(halves(received), axis=1)
        target = lax.broadcasted_iota(jnp.int32, (4 * length, 1), 0)
        component, along_index = split_index(target, length, 4)
        along_index = select(flip_along == 1, length - 1 - along_index, along_index)
        target = component * length + along_index
        swap = (lax.broadcasted_iota(jnp.int32, (4 * length, 4 * length), 1) == target)
        swap = swap.astype(jnp.float32).astype(jnp.bfloat16)
        both = jnp.dot(swap, both, preferred_element_type=jnp.float32).astype(jnp.bfloat16)

        def body(step, carry):
            start = pl.multiple_of(step * chunk, LANES)
            at = pl.ds(start, chunk)
            values = [padded[c, :, pl.ds(pl.multiple_of(start + LANES, LANES), chunk)] for c in range(4)]
            metric = [geometry[b, :, at] for b in range(3)]
            low_own, high_own = low_out[turn, :, at], high_out[turn, :, at]
            low_got, high_got = low_in[turn, :, at], high_in[turn, :, at]
            slopes, bends = [], []
            for c in range(4):
                ghosts = []
                for got, own, there in ((low_got, low_own, has_before), (high_got, high_own, has_after)):
                    for layer_index in range(2):
                        row = 2 * c + layer_index
                        ghosts.append(jnp.where(there, got[row:row + 1], -WALL[c] * own[row:row + 1]))
                low0, low1, high0, high1 = ghosts
                slope = jnp.where(row_of == 0, low1 - 8.0 * low0, 0.0)
                slope = jnp.where(row_of == 1, low0, slope)
                slope = jnp.where(row_of == length - 2, -high0, slope)
                slopes.append(jnp.where(row_of == length - 1, 8.0 * high0 - high1, slope))
                if c < 3:
                    bend = jnp.where(row_of == 0, 16.0 * low0 - low1, 0.0)
                    bend = jnp.where(row_of == 1, -low0, bend)
                    bend = jnp.where(row_of == length - 2, -high0, bend)
                    bends.append(jnp.where(row_of == length - 1, 16.0 * high0 - high1, bend))
            sums = rates_of(metric, values, slopes, bends)
            metric = [jnp.where(on_first, geometry[3 + b, :, at], geometry[6 + b, :, at]) for b in range(3)]
            slope = jnp.dot(both, slope_matrix[:, at], preferred_element_type=jnp.float32)
            bend = jnp.dot(both[:3 * length], bend_matrix[:, at], preferred_element_type=jnp.float32)
            slopes = [slope[c * length:(c + 1) * length] for c in range(4)]
            bends = [bend[c * length:(c + 1) * length] for c in range(3)]
            parts = rates_of(metric, values, slopes, bends)
            for c in range(4):
                finish(c, start, values[c], total[c, :, at] + sums[c] + parts[c])
            return carry

        lax.fori_loop(0, chunks, body, 0)

    def finish_first(c, start, value, rate):
        second[c, :, pl.ds(pl.multiple_of(start + LANES, LANES), chunk)] = value + (time_step / 12.0) * rate

    def finish_second(c, start, value, rate):
        base = first[c, :, pl.ds(pl.multiple_of(start + LANES, LANES), chunk)]
        out_ref[c, :, pl.ds(start, chunk)] = 0.5 * base + 0.5 * (value + (time_step / 12.0) * rate)

    load_state.wait()
    pack(first, 0)
    pl.semaphore_wait(barrier, segs - 1 + has_before.astype(jnp.int32) + has_after.astype(jnp.int32))

    start_chain(0)
    pack_face(first, 0)
    start_faces(0)
    build_spread()
    build_k()
    along_k()
    load_metric.wait()
    inside_rates(first)
    await_all(0)
    outside_rates(first, 0, finish_first)

    pack(second, 1)
    start_chain(1)
    pack_face(second, 1)
    start_faces(1)
    along_k()
    inside_rates(second)
    await_all(1)
    outside_rates(second, 1, finish_second)


def on_device(state, metric, block_map, links):
    segs, chain = lax.axis_size("seg"), lax.axis_size("blk")
    _, parts, length, width = state.shape
    cross = math.isqrt(width)
    chunk = math.lcm(cross, LANES)
    f32, bf16, dma = jnp.float32, jnp.bfloat16, pltpu.SemaphoreType.DMA
    result = pl.pallas_call(
        functools.partial(kernel, segs, chain, cross),
        out_shape=pltpu.VMEM((parts, length, width), f32),
        in_specs=[pl.BlockSpec(memory_space=pl.ANY)] * 2 + [pl.BlockSpec(memory_space=pltpu.SMEM)] * 2,
        out_specs=pl.BlockSpec(memory_space=pltpu.VMEM),
        scratch_shapes=[
            pltpu.VMEM((parts, length, width + 2 * LANES), f32),
            pltpu.VMEM((parts, length, width + 2 * LANES), f32),
            pltpu.VMEM((9, length, width), f32),
            pltpu.VMEM((parts, length, width), f32),
            pltpu.VMEM((width, LANES), bf16),
            pltpu.VMEM((2 * LANES, width), bf16),
            pltpu.VMEM((2 * LANES, width), bf16),
            pltpu.VMEM((2, parts * length, width), bf16),
            pltpu.VMEM((2 * chunk, chunk), bf16),
            pltpu.VMEM((2 * chunk, chunk), bf16),
            pltpu.VMEM((2 * chunk, chunk), bf16),
            pltpu.VMEM((parts, length, width), f32),
            pltpu.VMEM((parts - 1, length, width), f32),
            pltpu.VMEM((2, 2 * parts, width), f32),
            pltpu.VMEM((2, 2 * parts, width), f32),
            pltpu.VMEM((2, 2 * parts, width), f32),
            pltpu.VMEM((2, 2 * parts, width), f32),
            pltpu.VMEM((2, parts * length, LANES), f32),
            pltpu.VMEM((2, segs - 1, parts * length, LANES), f32),
            dma((2,)), dma((2, 2)), dma((2, 2)), dma((2, segs - 1)), dma((2, segs - 1)),
        ],
        compiler_params=pltpu.CompilerParams(collective_id=0, has_side_effects=True),
    )(state, metric, block_map, links.transpose(1, 2, 0))
    return result.reshape(state.shape)


def solution(mesh):
    in_specs = (P(("seg", "blk"), None, None, None), P(("seg", "blk"), None, None, None), P(), P())
    out_specs = P(("seg", "blk"), None, None, None)
    return jax.shard_map(
        on_device, mesh=mesh, in_specs=in_specs, out_specs=out_specs, check_vma=False
    )
```

```python
import functools
import math

import jax
import jax.numpy as jnp
from jax import lax
from jax.experimental import pallas as pl
from jax.experimental.pallas import tpu as pltpu
from jax.sharding import PartitionSpec as P

time_step = 0.05
viscosity = 0.2
compress = 1.0
MESH = pl.DeviceIdType.MESH
LANES = 128
WALL = (-1.0, -1.0, -1.0, 1.0)


def split_index(index, size, count):
    quotient = jnp.zeros_like(index)
    for step in range(1, count):
        quotient += (index >= size * step).astype(jnp.int32)
    return quotient, index - size * quotient


def halves(value):
    lead = value.astype(jnp.bfloat16)
    return lead, (value - lead.astype(jnp.float32)).astype(jnp.bfloat16)


def select(flag, yes, no):
    return jnp.where(flag, yes, no)


def kernel(segs, chain, cross, state_hbm, metric_hbm, block_map, links, out_ref,
           first, second, geometry, total, pack_matrix, slope_matrix, bend_matrix,
           split, k_slope_uvw, k_slope_p, k_bend, slope_k, bend_k,
           low_out, high_out, low_in, high_in, face_out, face_in,
           load_sem, chain_send, chain_recv, face_send, face_recv):
    length, width = out_ref.shape[1], out_ref.shape[2]
    chunk = math.lcm(cross, LANES)
    chunks = width // chunk
    inner = pl.ds(LANES, width)
    seg, pos = lax.axis_index("seg"), lax.axis_index("blk")
    me = seg * chain + pos
    has_before, has_after = pos > 0, pos < chain - 1
    before, after = lax.rem(pos + chain - 1, chain), lax.rem(pos + 1, chain)

    load_state = pltpu.make_async_copy(state_hbm.at[0], first.at[:, :, inner], load_sem.at[0])
    load_metric = pltpu.make_async_copy(metric_hbm.at[0], geometry, load_sem.at[1])
    load_state.start()
    load_metric.start()

    barrier = pltpu.get_barrier_semaphore()
    for offset in range(1, segs):
        pl.semaphore_signal(barrier, inc=1, device_id={"seg": lax.rem(seg + offset, segs)}, device_id_type=MESH)

    @pl.when(has_before)
    def _():
        pl.semaphore_signal(barrier, inc=1, device_id={"blk": before}, device_id_type=MESH)

    @pl.when(has_after)
    def _():
        pl.semaphore_signal(barrier, inc=1, device_id={"blk": after}, device_id_type=MESH)

    block = block_map[me]
    joins = [links[2 + side, 0, block] >= 0 for side in range(4)]
    partner, flip_along, flip_across = jnp.int32(-1), jnp.int32(0), jnp.int32(0)
    for side in range(4):
        partner = select(joins[side], links[2 + side, 0, block], partner)
        flip_along = select(joins[side], links[2 + side, 2, block], flip_along)
        flip_across = select(joins[side], links[2 + side, 3, block], flip_across)
    any_join = partner >= 0
    on_first = jnp.logical_or(joins[0], joins[1])
    on_high = jnp.logical_or(joins[1], joins[3])
    own_layers = [select(join, 0.0, 1.0) for join in joins]
    layer_stride = select(on_first, cross, 1)
    cell_stride = select(on_first, 1, cross)
    comes_from = []
    for offset in range(1, segs):
        device = lax.rem(seg + segs - offset, segs) * chain + pos
        comes_from.append(jnp.logical_and(any_join, block_map[device] == partner))

    pads = jnp.zeros((4, length, LANES), jnp.float32)
    for padded in (first, second):
        padded[:, :, :LANES] = pads
        padded[:, :, LANES + width:] = pads

    column = lax.broadcasted_iota(jnp.int32, (1, LANES), 1)
    layer, place = split_index(column, cross, 3)
    layer_place = select(on_high, cross - 1 - layer, layer)
    source = layer_place * layer_stride + place * cell_stride
    source = jnp.where(jnp.logical_and(layer < 2, any_join), source, -1)
    piece = 2 * LANES
    for part in range(width // piece):
        cells = lax.broadcasted_iota(jnp.int32, (piece, LANES), 0) + part * piece
        pack_matrix[part * piece:(part + 1) * piece, :] = (cells == source).astype(jnp.float32).astype(jnp.bfloat16)

    def pack(padded, turn):
        for c in range(4):
            for layer_index in range(2):
                row = 2 * c + layer_index
                low_out[turn, row:row + 1, :] = padded[c, layer_index:layer_index + 1, inner]
                high_out[turn, row:row + 1, :] = padded[c, length - 1 - layer_index:length - layer_index, inner]

    def pack_face(padded, turn):
        rows = 4 * length
        lead, trail = halves(padded[:, :, inner].reshape(rows, width))
        split[0] = lead
        split[1] = trail
        both = jnp.concatenate([lead, trail], axis=0)
        packed = jnp.dot(both, pack_matrix[...], preferred_element_type=jnp.float32)
        face_out[turn] = packed[:rows] + packed[rows:]

    def build_k():
        for matrix in (k_slope_uvw, k_slope_p, k_bend):
            matrix[...] = jnp.zeros((2 * chunk, chunk), jnp.bfloat16)
        low, high = own_layers[2], own_layers[3]
        here = lax.broadcasted_iota(jnp.int32, (cross, LANES), 0)
        column = lax.broadcasted_iota(jnp.int32, (cross, LANES), 1)
        for group in range(chunk // cross):
            first_row = group * cross
            for tile in range(first_row // LANES, (first_row + cross - 1) // LANES + 1):
                there = column + (tile * LANES - first_row)
                there = jnp.where(jnp.logical_and(there >= 0, there < cross), there, 4 * width)
                offset, mirrored = here - there, here + there

                def at(index, value, factor):
                    return jnp.where(index == value, factor, 0.0)

                slope = at(offset, -2, 1.0) + at(offset, -1, -8.0) + at(offset, 1, 8.0) + at(offset, 2, -1.0)
                bend = (at(offset, -2, -1.0) + at(offset, -1, 16.0) + at(offset, 0, -30.0)
                        + at(offset, 1, 16.0) + at(offset, 2, -1.0))
                end = 2 * cross - 2
                wall_slope = (at(mirrored, 0, -8.0 * low) + at(mirrored, 1, low)
                              + at(mirrored, end, 8.0 * high) + at(mirrored, end - 1, -high))
                wall_bend = (at(mirrored, 0, 16.0 * low) + at(mirrored, 1, -low)
                             + at(mirrored, end, 16.0 * high) + at(mirrored, end - 1, -high))
                lanes = slice(tile * LANES, (tile + 1) * LANES)
                for matrix, value in ((k_slope_uvw, slope + WALL[0] * wall_slope),
                                      (k_slope_p, slope + WALL[3] * wall_slope),
                                      (k_bend, bend + WALL[0] * wall_bend)):
                    value = value.astype(jnp.bfloat16)
                    matrix[first_row:first_row + cross, lanes] = value
                    matrix[chunk + first_row:chunk + first_row + cross, lanes] = value

    def along_k():
        rows = 3 * length
        parts = []
        for step in range(chunks):
            at = slice(step * chunk, (step + 1) * chunk)
            parts.append(jnp.concatenate([split[0, :, at], split[1, :, at]], axis=1))
        velocity = jnp.concatenate([part[:rows] for part in parts], axis=0)
        pressure = jnp.concatenate([part[rows:] for part in parts], axis=0)
        slope = jnp.dot(velocity, k_slope_uvw[...], preferred_element_type=jnp.float32)
        bend = jnp.dot(velocity, k_bend[...], preferred_element_type=jnp.float32)
        slope_p = jnp.dot(pressure, k_slope_p[...], preferred_element_type=jnp.float32)
        for step in range(chunks):
            at = slice(step * chunk, (step + 1) * chunk)
            slope_k[:3, :, at] = slope[step * rows:(step + 1) * rows].reshape(3, length, chunk)
            bend_k[:, :, at] = bend[step * rows:(step + 1) * rows].reshape(3, length, chunk)
            slope_k[3, :, at] = slope_p[step * length:(step + 1) * length]

    def chain_copies(turn):
        to_before = pltpu.make_async_remote_copy(
            low_out.at[turn], high_in.at[turn], chain_send.at[turn, 0], chain_recv.at[turn, 0],
            device_id={"blk": before}, device_id_type=MESH)
        to_after = pltpu.make_async_remote_copy(
            high_out.at[turn], low_in.at[turn], chain_send.at[turn, 1], chain_recv.at[turn, 1],
            device_id={"blk": after}, device_id_type=MESH)
        return to_before, to_after

    def face_copies(turn):
        return [pltpu.make_async_remote_copy(
            face_out.at[turn], face_in.at[turn, offset - 1], face_send.at[turn, offset - 1],
            face_recv.at[turn, offset - 1], device_id={"seg": lax.rem(seg + offset, segs)}, device_id_type=MESH)
            for offset in range(1, segs)]

    def start_chain(turn):
        to_before, to_after = chain_copies(turn)

        @pl.when(has_before)
        def _():
            to_before.start()

        @pl.when(has_after)
        def _():
            to_after.start()

    def start_faces(turn):
        for copy in face_copies(turn):
            copy.start()

    def await_chain(turn):
        to_before, to_after = chain_copies(turn)

        @pl.when(has_before)
        def _():
            to_before.wait_send()
            to_after.wait_recv()

        @pl.when(has_after)
        def _():
            to_after.wait_send()
            to_before.wait_recv()

    def await_faces(turn):
        for copy in face_copies(turn):
            copy.wait()

    def build_spread():
        row = lax.broadcasted_iota(jnp.int32, (LANES, 1), 0)
        layer, place = split_index(row, cross, 3)
        place = select(flip_across == 1, cross - 1 - place, place)
        valid = jnp.logical_and(layer < 2, any_join)
        near = select(on_high, cross - 1, 0)
        spot = select(on_high, cross - 2 + layer, 1 - layer)
        outer = jnp.where(valid, spot * layer_stride + place * cell_stride, -1)
        edge = jnp.where(jnp.logical_and(valid, layer == 0), near * layer_stride + place * cell_stride, -1)
        sign = select(on_high, -1.0, 1.0)
        for part in range(width // LANES):
            cells = lax.broadcasted_iota(jnp.int32, (LANES, LANES), 1) + part * LANES
            is_outer = (cells == outer).astype(jnp.float32)
            is_edge = (cells == edge).astype(jnp.float32)
            slope = (sign * (is_outer - 8.0 * is_edge)).astype(jnp.bfloat16)
            bend = (16.0 * is_edge - is_outer).astype(jnp.bfloat16)
            at = slice(part * LANES, (part + 1) * LANES)
            slope_matrix[:LANES, at] = slope
            slope_matrix[LANES:, at] = slope
            bend_matrix[:LANES, at] = bend
            bend_matrix[LANES:, at] = bend

    lane = lax.broadcasted_iota(jnp.int32, (length, chunk), 1)
    row_of = lax.broadcasted_iota(jnp.int32, (length, chunk), 0)

    def central(value, minus2, minus1, plus1, plus2, bent):
        slope = (minus2 - plus2) + 8.0 * (plus1 - minus1)
        if not bent:
            return slope, None
        return slope, 16.0 * (minus1 + plus1) - (minus2 + plus2) - 30.0 * value

    def along(value, bent):
        def moved(step):
            rolled = pltpu.roll(value, step % length, 0)
            inside = row_of >= step if step > 0 else row_of < length + step
            return jnp.where(inside, rolled, 0.0)
        return central(value, moved(2), moved(1), moved(-1), moved(-2), bent)

    def along_j(wide, value, low_factor, high_factor, bent):
        def moved(step):
            if step > 0:
                return pltpu.roll(wide[:, :LANES + chunk], step, 1)[:, LANES:]
            return pltpu.roll(wide[:, LANES:], LANES + chunk + step, 1)[:, :chunk]
        minus2, minus1, plus1, plus2 = moved(2 * cross), moved(cross), moved(-cross), moved(-2 * cross)
        m1, m2, p1, p2 = minus1, minus2, plus1, plus2
        if low_factor is not None:
            m1 = jnp.where(lane < cross, low_factor * value, minus1)
            m2 = jnp.where(lane < cross, low_factor * plus1, jnp.where(lane < 2 * cross, low_factor * minus1, minus2))
        if high_factor is not None:
            p1 = jnp.where(lane >= chunk - cross, high_factor * value, plus1)
            p2 = jnp.where(lane >= chunk - cross, high_factor * minus1,
                           jnp.where(lane >= chunk - 2 * cross, high_factor * plus1, plus2))
        return central(value, m2, m1, p1, p2, bent)

    def weights(metric, values):
        carried = metric[0] * values[0] + metric[1] * values[1] + metric[2] * values[2]
        norm = viscosity * (metric[0] * metric[0] + metric[1] * metric[1] + metric[2] * metric[2])
        return carried, norm

    def rates_of(metric, values, slopes, bends):
        carried, norm = weights(metric, values)
        parts = [norm * bends[c] - carried * slopes[c] - metric[c] * slopes[3] for c in range(3)]
        parts.append(-compress * (metric[0] * slopes[0] + metric[1] * slopes[1] + metric[2] * slopes[2]))
        return parts

    def inside_rates(padded):
        def at_chunk(start, is_first, is_last):
            at = pl.ds(start, chunk)
            wide = [padded[c, :, pl.ds(start, chunk + 2 * LANES)] for c in range(4)]
            values = [w[:, LANES:LANES + chunk] for w in wide]
            sums = None
            for direction in range(3):
                metric = [geometry[3 * direction + b, :, at] for b in range(3)]
                if direction == 2:
                    slopes = [slope_k[c, :, at] for c in range(4)]
                    bends = [bend_k[c, :, at] for c in range(3)]
                else:
                    slopes, bends = [], []
                    for c in range(4):
                        if direction == 0:
                            slope, bend = along(values[c], c < 3)
                        else:
                            low = WALL[c] * own_layers[0] if is_first else None
                            high = WALL[c] * own_layers[1] if is_last else None
                            slope, bend = along_j(wide[c], values[c], low, high, c < 3)
                        slopes.append(slope)
                        bends.append(bend)
                parts = rates_of(metric, values, slopes, bends)
                sums = parts if sums is None else [a + b for a, b in zip(sums, parts)]
            for c in range(4):
                total[c, :, at] = sums[c]

        at_chunk(0, True, chunks == 1)
        if chunks > 2:
            @pl.loop(1, chunks - 1)
            def _(step):
                at_chunk(pl.multiple_of(step * chunk, LANES), False, False)
        if chunks > 1:
            at_chunk((chunks - 1) * chunk, False, True)

    def chain_rates(padded, turn):
        def body(step, carry):
            start = pl.multiple_of(step * chunk, LANES)
            at = pl.ds(start, chunk)
            values = [padded[c, :, pl.ds(pl.multiple_of(start + LANES, LANES), chunk)] for c in range(4)]
            metric = [geometry[b, :, at] for b in range(3)]
            low_own, high_own = low_out[turn, :, at], high_out[turn, :, at]
            low_got, high_got = low_in[turn, :, at], high_in[turn, :, at]
            slopes, bends = [], []
            for c in range(4):
                ghosts = []
                for got, own, there in ((low_got, low_own, has_before), (high_got, high_own, has_after)):
                    for layer_index in range(2):
                        row = 2 * c + layer_index
                        ghosts.append(jnp.where(there, got[row:row + 1], -WALL[c] * own[row:row + 1]))
                low0, low1, high0, high1 = ghosts
                slope = jnp.where(row_of == 0, low1 - 8.0 * low0, 0.0)
                slope = jnp.where(row_of == 1, low0, slope)
                slope = jnp.where(row_of == length - 2, -high0, slope)
                slopes.append(jnp.where(row_of == length - 1, 8.0 * high0 - high1, slope))
                if c < 3:
                    bend = jnp.where(row_of == 0, 16.0 * low0 - low1, 0.0)
                    bend = jnp.where(row_of == 1, -low0, bend)
                    bend = jnp.where(row_of == length - 2, -high0, bend)
                    bends.append(jnp.where(row_of == length - 1, 16.0 * high0 - high1, bend))
            sums = rates_of(metric, values, slopes, bends)
            for c in range(4):
                total[c, :, at] += sums[c]
            return carry

        lax.fori_loop(0, chunks, body, 0)

    def face_rates(padded, turn, finish):
        received = jnp.zeros((4 * length, LANES), jnp.float32)
        for index, here in enumerate(comes_from):
            received = jnp.where(here, face_in[turn, index], received)
        both = jnp.concatenate(halves(received), axis=1)
        target = lax.broadcasted_iota(jnp.int32, (4 * length, 1), 0)
        component, along_index = split_index(target, length, 4)
        along_index = select(flip_along == 1, length - 1 - along_index, along_index)
        target = component * length + along_index
        swap = (lax.broadcasted_iota(jnp.int32, (4 * length, 4 * length), 1) == target)
        swap = swap.astype(jnp.float32).astype(jnp.bfloat16)
        both = jnp.dot(swap, both, preferred_element_type=jnp.float32).astype(jnp.bfloat16)

        def body(step, carry):
            start = pl.multiple_of(step * chunk, LANES)
            at = pl.ds(start, chunk)
            values = [padded[c, :, pl.ds(pl.multiple_of(start + LANES, LANES), chunk)] for c in range(4)]
            metric = [jnp.where(on_first, geometry[3 + b, :, at], geometry[6 + b, :, at]) for b in range(3)]
            slope = jnp.dot(both, slope_matrix[:, at], preferred_element_type=jnp.float32)
            bend = jnp.dot(both[:3 * length], bend_matrix[:, at], preferred_element_type=jnp.float32)
            slopes = [slope[c * length:(c + 1) * length] for c in range(4)]
            bends = [bend[c * length:(c + 1) * length] for c in range(3)]
            parts = rates_of(metric, values, slopes, bends)
            for c in range(4):
                finish(c, start, values[c], total[c, :, at] + parts[c])
            return carry

        lax.fori_loop(0, chunks, body, 0)

    def finish_first(c, start, value, rate):
        second[c, :, pl.ds(pl.multiple_of(start + LANES, LANES), chunk)] = value + (time_step / 12.0) * rate

    def finish_second(c, start, value, rate):
        base = first[c, :, pl.ds(pl.multiple_of(start + LANES, LANES), chunk)]
        out_ref[c, :, pl.ds(start, chunk)] = 0.5 * base + 0.5 * (value + (time_step / 12.0) * rate)

    load_state.wait()
    pack_face(first, 0)
    pl.semaphore_wait(barrier, segs - 1 + has_before.astype(jnp.int32) + has_after.astype(jnp.int32))

    start_faces(0)
    pack(first, 0)
    start_chain(0)
    build_spread()
    build_k()
    along_k()
    load_metric.wait()
    inside_rates(first)
    await_chain(0)
    chain_rates(first, 0)
    await_faces(0)
    face_rates(first, 0, finish_first)

    pack_face(second, 1)
    start_faces(1)
    pack(second, 1)
    start_chain(1)
    along_k()
    inside_rates(second)
    await_chain(1)
    chain_rates(second, 1)
    await_faces(1)
    face_rates(second, 1, finish_second)


def on_device(state, metric, block_map, links):
    segs, chain = lax.axis_size("seg"), lax.axis_size("blk")
    _, parts, length, width = state.shape
    cross = math.isqrt(width)
    chunk = math.lcm(cross, LANES)
    f32, bf16, dma = jnp.float32, jnp.bfloat16, pltpu.SemaphoreType.DMA
    result = pl.pallas_call(
        functools.partial(kernel, segs, chain, cross),
        out_shape=pltpu.VMEM((parts, length, width), f32),
        in_specs=[pl.BlockSpec(memory_space=pl.ANY)] * 2 + [pl.BlockSpec(memory_space=pltpu.SMEM)] * 2,
        out_specs=pl.BlockSpec(memory_space=pltpu.VMEM),
        scratch_shapes=[
            pltpu.VMEM((parts, length, width + 2 * LANES), f32),
            pltpu.VMEM((parts, length, width + 2 * LANES), f32),
            pltpu.VMEM((9, length, width), f32),
            pltpu.VMEM((parts, length, width), f32),
            pltpu.VMEM((width, LANES), bf16),
            pltpu.VMEM((2 * LANES, width), bf16),
            pltpu.VMEM((2 * LANES, width), bf16),
            pltpu.VMEM((2, parts * length, width), bf16),
            pltpu.VMEM((2 * chunk, chunk), bf16),
            pltpu.VMEM((2 * chunk, chunk), bf16),
            pltpu.VMEM((2 * chunk, chunk), bf16),
            pltpu.VMEM((parts, length, width), f32),
            pltpu.VMEM((parts - 1, length, width), f32),
            pltpu.VMEM((2, 2 * parts, width), f32),
            pltpu.VMEM((2, 2 * parts, width), f32),
            pltpu.VMEM((2, 2 * parts, width), f32),
            pltpu.VMEM((2, 2 * parts, width), f32),
            pltpu.VMEM((2, parts * length, LANES), f32),
            pltpu.VMEM((2, segs - 1, parts * length, LANES), f32),
            dma((2,)), dma((2, 2)), dma((2, 2)), dma((2, segs - 1)), dma((2, segs - 1)),
        ],
        compiler_params=pltpu.CompilerParams(collective_id=0, has_side_effects=True),
    )(state, metric, block_map, links.transpose(1, 2, 0))
    return result.reshape(state.shape)


def solution(mesh):
    in_specs = (P(("seg", "blk"), None, None, None), P(("seg", "blk"), None, None, None), P(), P())
    out_specs = P(("seg", "blk"), None, None, None)
    return jax.shard_map(
        on_device, mesh=mesh, in_specs=in_specs, out_specs=out_specs, check_vma=False
    )
```

```python
import functools
import math

import jax
import jax.numpy as jnp
from jax import lax
from jax.experimental import pallas as pl
from jax.experimental.pallas import tpu as pltpu
from jax.sharding import PartitionSpec as P

time_step = 0.05
viscosity = 0.2
compress = 1.0
MESH = pl.DeviceIdType.MESH
LANES = 128
WALL = (-1.0, -1.0, -1.0, 1.0)


def split_index(index, size, count):
    quotient = jnp.zeros_like(index)
    for step in range(1, count):
        quotient += (index >= size * step).astype(jnp.int32)
    return quotient, index - size * quotient


def halves(value):
    lead = value.astype(jnp.bfloat16)
    return lead, (value - lead.astype(jnp.float32)).astype(jnp.bfloat16)


def select(flag, yes, no):
    return jnp.where(flag, yes, no)


def kernel(segs, chain, cross, state_hbm, metric_hbm, block_map, links, out_ref,
           first, second, geometry, total, pack_matrix, slope_matrix, bend_matrix,
           split, k_slope_uvw, k_slope_p, k_bend, slope_k, bend_k,
           low_out, high_out, low_in, high_in, face_out, face_in,
           load_sem, chain_send, chain_recv, face_send, face_recv):
    length, width = out_ref.shape[1], out_ref.shape[2]
    chunk = math.lcm(cross, LANES)
    chunks = width // chunk
    inner = pl.ds(LANES, width)
    seg, pos = lax.axis_index("seg"), lax.axis_index("blk")
    me = seg * chain + pos
    has_before, has_after = pos > 0, pos < chain - 1
    before, after = lax.rem(pos + chain - 1, chain), lax.rem(pos + 1, chain)

    load_state = pltpu.make_async_copy(state_hbm.at[0], first.at[:, :, inner], load_sem.at[0])
    load_metric = pltpu.make_async_copy(metric_hbm.at[0], geometry, load_sem.at[1])
    load_state.start()
    load_metric.start()

    barrier = pltpu.get_barrier_semaphore()
    for offset in range(1, segs):
        pl.semaphore_signal(barrier, inc=1, device_id={"seg": lax.rem(seg + offset, segs)}, device_id_type=MESH)

    @pl.when(has_before)
    def _():
        pl.semaphore_signal(barrier, inc=1, device_id={"blk": before}, device_id_type=MESH)

    @pl.when(has_after)
    def _():
        pl.semaphore_signal(barrier, inc=1, device_id={"blk": after}, device_id_type=MESH)

    block = block_map[me]
    joins = [links[2 + side, 0, block] >= 0 for side in range(4)]
    partner, flip_along, flip_across = jnp.int32(-1), jnp.int32(0), jnp.int32(0)
    for side in range(4):
        partner = select(joins[side], links[2 + side, 0, block], partner)
        flip_along = select(joins[side], links[2 + side, 2, block], flip_along)
        flip_across = select(joins[side], links[2 + side, 3, block], flip_across)
    any_join = partner >= 0
    on_first = jnp.logical_or(joins[0], joins[1])
    on_high = jnp.logical_or(joins[1], joins[3])
    own_layers = [select(join, 0.0, 1.0) for join in joins]
    layer_stride = select(on_first, cross, 1)
    cell_stride = select(on_first, 1, cross)
    comes_from = []
    for offset in range(1, segs):
        device = lax.rem(seg + segs - offset, segs) * chain + pos
        comes_from.append(jnp.logical_and(any_join, block_map[device] == partner))

    pads = jnp.zeros((4, length, LANES), jnp.float32)
    for padded in (first, second):
        padded[:, :, :LANES] = pads
        padded[:, :, LANES + width:] = pads

    column = lax.broadcasted_iota(jnp.int32, (1, LANES), 1)
    layer, place = split_index(column, cross, 3)
    layer_place = select(on_high, cross - 1 - layer, layer)
    source = layer_place * layer_stride + place * cell_stride
    source = jnp.where(jnp.logical_and(layer < 2, any_join), source, -1)
    piece = 2 * LANES
    for part in range(width // piece):
        cells = lax.broadcasted_iota(jnp.int32, (piece, LANES), 0) + part * piece
        pack_matrix[part * piece:(part + 1) * piece, :] = (cells == source).astype(jnp.float32).astype(jnp.bfloat16)

    def pack(padded, turn):
        for c in range(4):
            for layer_index in range(2):
                row = 2 * c + layer_index
                low_out[turn, row:row + 1, :] = padded[c, layer_index:layer_index + 1, inner]
                high_out[turn, row:row + 1, :] = padded[c, length - 1 - layer_index:length - layer_index, inner]

    def pack_face(padded, turn):
        rows = 4 * length
        lead, trail = halves(padded[:, :, inner].reshape(rows, width))
        split[0] = lead
        split[1] = trail
        both = jnp.concatenate([lead, trail], axis=0)
        packed = jnp.dot(both, pack_matrix[...], preferred_element_type=jnp.float32)
        face_out[turn] = packed[:rows] + packed[rows:]

    def build_k():
        low, high = own_layers[2], own_layers[3]
        here = lax.broadcasted_iota(jnp.int32, (cross, LANES), 0)
        column = lax.broadcasted_iota(jnp.int32, (cross, LANES), 1)
        for group in range(chunk // cross):
            first_row = group * cross
            for tile in range(chunk // LANES):
                lanes = slice(tile * LANES, (tile + 1) * LANES)
                if not first_row // LANES <= tile <= (first_row + cross - 1) // LANES:
                    for matrix in (k_slope_uvw, k_slope_p, k_bend):
                        for top in (first_row, chunk + first_row):
                            matrix[top:top + cross, lanes] = jnp.zeros((cross, LANES), jnp.bfloat16)
                    continue
                there = column + (tile * LANES - first_row)
                there = jnp.where(jnp.logical_and(there >= 0, there < cross), there, 4 * width)
                offset, mirrored = here - there, here + there

                def at(index, value, factor):
                    return jnp.where(index == value, factor, 0.0)

                slope = at(offset, -2, 1.0) + at(offset, -1, -8.0) + at(offset, 1, 8.0) + at(offset, 2, -1.0)
                bend = (at(offset, -2, -1.0) + at(offset, -1, 16.0) + at(offset, 0, -30.0)
                        + at(offset, 1, 16.0) + at(offset, 2, -1.0))
                end = 2 * cross - 2
                wall_slope = (at(mirrored, 0, -8.0 * low) + at(mirrored, 1, low)
                              + at(mirrored, end, 8.0 * high) + at(mirrored, end - 1, -high))
                wall_bend = (at(mirrored, 0, 16.0 * low) + at(mirrored, 1, -low)
                             + at(mirrored, end, 16.0 * high) + at(mirrored, end - 1, -high))
                for matrix, value in ((k_slope_uvw, slope + WALL[0] * wall_slope),
                                      (k_slope_p, slope + WALL[3] * wall_slope),
                                      (k_bend, bend + WALL[0] * wall_bend)):
                    value = value.astype(jnp.bfloat16)
                    matrix[first_row:first_row + cross, lanes] = value
                    matrix[chunk + first_row:chunk + first_row + cross, lanes] = value

    def along_k():
        rows = 3 * length
        parts = []
        for step in range(chunks):
            at = slice(step * chunk, (step + 1) * chunk)
            parts.append(jnp.concatenate([split[0, :, at], split[1, :, at]], axis=1))
        velocity = jnp.concatenate([part[:rows] for part in parts], axis=0)
        pressure = jnp.concatenate([part[rows:] for part in parts], axis=0)
        slope = jnp.dot(velocity, k_slope_uvw[...], preferred_element_type=jnp.float32)
        bend = jnp.dot(velocity, k_bend[...], preferred_element_type=jnp.float32)
        slope_p = jnp.dot(pressure, k_slope_p[...], preferred_element_type=jnp.float32)
        for step in range(chunks):
            at = slice(step * chunk, (step + 1) * chunk)
            slope_k[:3, :, at] = slope[step * rows:(step + 1) * rows].reshape(3, length, chunk)
            bend_k[:, :, at] = bend[step * rows:(step + 1) * rows].reshape(3, length, chunk)
            slope_k[3, :, at] = slope_p[step * length:(step + 1) * length]

    def chain_copies(turn):
        to_before = pltpu.make_async_remote_copy(
            low_out.at[turn], high_in.at[turn], chain_send.at[turn, 0], chain_recv.at[turn, 0],
            device_id={"blk": before}, device_id_type=MESH)
        to_after = pltpu.make_async_remote_copy(
            high_out.at[turn], low_in.at[turn], chain_send.at[turn, 1], chain_recv.at[turn, 1],
            device_id={"blk": after}, device_id_type=MESH)
        return to_before, to_after

    def face_copies(turn):
        return [pltpu.make_async_remote_copy(
            face_out.at[turn], face_in.at[turn, offset - 1], face_send.at[turn, offset - 1],
            face_recv.at[turn, offset - 1], device_id={"seg": lax.rem(seg + offset, segs)}, device_id_type=MESH)
            for offset in range(1, segs)]

    def start_chain(turn):
        to_before, to_after = chain_copies(turn)

        @pl.when(has_before)
        def _():
            to_before.start()

        @pl.when(has_after)
        def _():
            to_after.start()

    def start_faces(turn):
        for copy in face_copies(turn):
            copy.start()

    def await_chain(turn):
        to_before, to_after = chain_copies(turn)

        @pl.when(has_before)
        def _():
            to_before.wait_send()
            to_after.wait_recv()

        @pl.when(has_after)
        def _():
            to_after.wait_send()
            to_before.wait_recv()

    def await_faces(turn):
        for copy in face_copies(turn):
            copy.wait()

    def build_spread():
        row = lax.broadcasted_iota(jnp.int32, (LANES, 1), 0)
        layer, place = split_index(row, cross, 3)
        place = select(flip_across == 1, cross - 1 - place, place)
        valid = jnp.logical_and(layer < 2, any_join)
        near = select(on_high, cross - 1, 0)
        spot = select(on_high, cross - 2 + layer, 1 - layer)
        outer = jnp.where(valid, spot * layer_stride + place * cell_stride, -1)
        edge = jnp.where(jnp.logical_and(valid, layer == 0), near * layer_stride + place * cell_stride, -1)
        sign = select(on_high, -1.0, 1.0)
        for part in range(width // LANES):
            cells = lax.broadcasted_iota(jnp.int32, (LANES, LANES), 1) + part * LANES
            is_outer = (cells == outer).astype(jnp.float32)
            is_edge = (cells == edge).astype(jnp.float32)
            slope = (sign * (is_outer - 8.0 * is_edge)).astype(jnp.bfloat16)
            bend = (16.0 * is_edge - is_outer).astype(jnp.bfloat16)
            at = slice(part * LANES, (part + 1) * LANES)
            slope_matrix[:LANES, at] = slope
            slope_matrix[LANES:, at] = slope
            bend_matrix[:LANES, at] = bend
            bend_matrix[LANES:, at] = bend

    lane = lax.broadcasted_iota(jnp.int32, (length, chunk), 1)
    row_of = lax.broadcasted_iota(jnp.int32, (length, chunk), 0)

    def central(value, minus2, minus1, plus1, plus2, bent):
        slope = (minus2 - plus2) + 8.0 * (plus1 - minus1)
        if not bent:
            return slope, None
        return slope, 16.0 * (minus1 + plus1) - (minus2 + plus2) - 30.0 * value

    def along(value, bent):
        def moved(step):
            rolled = pltpu.roll(value, step % length, 0)
            inside = row_of >= step if step > 0 else row_of < length + step
            return jnp.where(inside, rolled, 0.0)
        return central(value, moved(2), moved(1), moved(-1), moved(-2), bent)

    def along_j(wide, value, low_factor, high_factor, bent):
        def moved(step):
            if step > 0:
                return pltpu.roll(wide[:, :LANES + chunk], step, 1)[:, LANES:]
            return pltpu.roll(wide[:, LANES:], LANES + chunk + step, 1)[:, :chunk]
        minus2, minus1, plus1, plus2 = moved(2 * cross), moved(cross), moved(-cross), moved(-2 * cross)
        m1, m2, p1, p2 = minus1, minus2, plus1, plus2
        if low_factor is not None:
            m1 = jnp.where(lane < cross, low_factor * value, minus1)
            m2 = jnp.where(lane < cross, low_factor * plus1, jnp.where(lane < 2 * cross, low_factor * minus1, minus2))
        if high_factor is not None:
            p1 = jnp.where(lane >= chunk - cross, high_factor * value, plus1)
            p2 = jnp.where(lane >= chunk - cross, high_factor * minus1,
                           jnp.where(lane >= chunk - 2 * cross, high_factor * plus1, plus2))
        return central(value, m2, m1, p1, p2, bent)

    def weights(metric, values):
        carried = metric[0] * values[0] + metric[1] * values[1] + metric[2] * values[2]
        norm = viscosity * (metric[0] * metric[0] + metric[1] * metric[1] + metric[2] * metric[2])
        return carried, norm

    def rates_of(metric, values, slopes, bends):
        carried, norm = weights(metric, values)
        parts = [norm * bends[c] - carried * slopes[c] - metric[c] * slopes[3] for c in range(3)]
        parts.append(-compress * (metric[0] * slopes[0] + metric[1] * slopes[1] + metric[2] * slopes[2]))
        return parts

    def inside_rates(padded):
        def at_chunk(start, is_first, is_last):
            at = pl.ds(start, chunk)
            wide = [padded[c, :, pl.ds(start, chunk + 2 * LANES)] for c in range(4)]
            values = [w[:, LANES:LANES + chunk] for w in wide]
            sums = None
            for direction in range(3):
                metric = [geometry[3 * direction + b, :, at] for b in range(3)]
                if direction == 2:
                    slopes = [slope_k[c, :, at] for c in range(4)]
                    bends = [bend_k[c, :, at] for c in range(3)]
                else:
                    slopes, bends = [], []
                    for c in range(4):
                        if direction == 0:
                            slope, bend = along(values[c], c < 3)
                        else:
                            low = WALL[c] * own_layers[0] if is_first else None
                            high = WALL[c] * own_layers[1] if is_last else None
                            slope, bend = along_j(wide[c], values[c], low, high, c < 3)
                        slopes.append(slope)
                        bends.append(bend)
                parts = rates_of(metric, values, slopes, bends)
                sums = parts if sums is None else [a + b for a, b in zip(sums, parts)]
            for c in range(4):
                total[c, :, at] = sums[c]

        at_chunk(0, True, chunks == 1)
        if chunks > 2:
            @pl.loop(1, chunks - 1)
            def _(step):
                at_chunk(pl.multiple_of(step * chunk, LANES), False, False)
        if chunks > 1:
            at_chunk((chunks - 1) * chunk, False, True)

    def chain_rates(padded, turn):
        def body(step, carry):
            start = pl.multiple_of(step * chunk, LANES)
            at = pl.ds(start, chunk)
            values = [padded[c, :, pl.ds(pl.multiple_of(start + LANES, LANES), chunk)] for c in range(4)]
            metric = [geometry[b, :, at] for b in range(3)]
            low_own, high_own = low_out[turn, :, at], high_out[turn, :, at]
            low_got, high_got = low_in[turn, :, at], high_in[turn, :, at]
            slopes, bends = [], []
            for c in range(4):
                ghosts = []
                for got, own, there in ((low_got, low_own, has_before), (high_got, high_own, has_after)):
                    for layer_index in range(2):
                        row = 2 * c + layer_index
                        ghosts.append(jnp.where(there, got[row:row + 1], -WALL[c] * own[row:row + 1]))
                low0, low1, high0, high1 = ghosts
                slope = jnp.where(row_of == 0, low1 - 8.0 * low0, 0.0)
                slope = jnp.where(row_of == 1, low0, slope)
                slope = jnp.where(row_of == length - 2, -high0, slope)
                slopes.append(jnp.where(row_of == length - 1, 8.0 * high0 - high1, slope))
                if c < 3:
                    bend = jnp.where(row_of == 0, 16.0 * low0 - low1, 0.0)
                    bend = jnp.where(row_of == 1, -low0, bend)
                    bend = jnp.where(row_of == length - 2, -high0, bend)
                    bends.append(jnp.where(row_of == length - 1, 16.0 * high0 - high1, bend))
            sums = rates_of(metric, values, slopes, bends)
            for c in range(4):
                total[c, :, at] += sums[c]
            return carry

        lax.fori_loop(0, chunks, body, 0)

    def face_rates(padded, turn, finish):
        received = jnp.zeros((4 * length, LANES), jnp.float32)
        for index, here in enumerate(comes_from):
            received = jnp.where(here, face_in[turn, index], received)
        both = jnp.concatenate(halves(received), axis=1)
        target = lax.broadcasted_iota(jnp.int32, (4 * length, 1), 0)
        component, along_index = split_index(target, length, 4)
        along_index = select(flip_along == 1, length - 1 - along_index, along_index)
        target = component * length + along_index
        swap = (lax.broadcasted_iota(jnp.int32, (4 * length, 4 * length), 1) == target)
        swap = swap.astype(jnp.float32).astype(jnp.bfloat16)
        both = jnp.dot(swap, both, preferred_element_type=jnp.float32).astype(jnp.bfloat16)

        def body(step, carry):
            start = pl.multiple_of(step * chunk, LANES)
            at = pl.ds(start, chunk)
            values = [padded[c, :, pl.ds(pl.multiple_of(start + LANES, LANES), chunk)] for c in range(4)]
            metric = [jnp.where(on_first, geometry[3 + b, :, at], geometry[6 + b, :, at]) for b in range(3)]
            slope = jnp.dot(both, slope_matrix[:, at], preferred_element_type=jnp.float32)
            bend = jnp.dot(both[:3 * length], bend_matrix[:, at], preferred_element_type=jnp.float32)
            slopes = [slope[c * length:(c + 1) * length] for c in range(4)]
            bends = [bend[c * length:(c + 1) * length] for c in range(3)]
            parts = rates_of(metric, values, slopes, bends)
            for c in range(4):
                finish(c, start, values[c], total[c, :, at] + parts[c])
            return carry

        lax.fori_loop(0, chunks, body, 0)

    def finish_first(c, start, value, rate):
        second[c, :, pl.ds(pl.multiple_of(start + LANES, LANES), chunk)] = value + (time_step / 12.0) * rate

    def finish_second(c, start, value, rate):
        base = first[c, :, pl.ds(pl.multiple_of(start + LANES, LANES), chunk)]
        out_ref[c, :, pl.ds(start, chunk)] = 0.5 * base + 0.5 * (value + (time_step / 12.0) * rate)

    build_spread()
    build_k()
    load_state.wait()
    pack_face(first, 0)
    pl.semaphore_wait(barrier, segs - 1 + has_before.astype(jnp.int32) + has_after.astype(jnp.int32))

    start_faces(0)
    pack(first, 0)
    start_chain(0)
    along_k()
    load_metric.wait()
    inside_rates(first)
    await_chain(0)
    chain_rates(first, 0)
    await_faces(0)
    face_rates(first, 0, finish_first)

    pack_face(second, 1)
    start_faces(1)
    pack(second, 1)
    start_chain(1)
    along_k()
    inside_rates(second)
    await_chain(1)
    chain_rates(second, 1)
    await_faces(1)
    face_rates(second, 1, finish_second)


def on_device(state, metric, block_map, links):
    segs, chain = lax.axis_size("seg"), lax.axis_size("blk")
    _, parts, length, width = state.shape
    cross = math.isqrt(width)
    chunk = math.lcm(cross, LANES)
    f32, bf16, dma = jnp.float32, jnp.bfloat16, pltpu.SemaphoreType.DMA
    result = pl.pallas_call(
        functools.partial(kernel, segs, chain, cross),
        out_shape=pltpu.VMEM((parts, length, width), f32),
        in_specs=[pl.BlockSpec(memory_space=pl.ANY)] * 2 + [pl.BlockSpec(memory_space=pltpu.SMEM)] * 2,
        out_specs=pl.BlockSpec(memory_space=pltpu.VMEM),
        scratch_shapes=[
            pltpu.VMEM((parts, length, width + 2 * LANES), f32),
            pltpu.VMEM((parts, length, width + 2 * LANES), f32),
            pltpu.VMEM((9, length, width), f32),
            pltpu.VMEM((parts, length, width), f32),
            pltpu.VMEM((width, LANES), bf16),
            pltpu.VMEM((2 * LANES, width), bf16),
            pltpu.VMEM((2 * LANES, width), bf16),
            pltpu.VMEM((2, parts * length, width), bf16),
            pltpu.VMEM((2 * chunk, chunk), bf16),
            pltpu.VMEM((2 * chunk, chunk), bf16),
            pltpu.VMEM((2 * chunk, chunk), bf16),
            pltpu.VMEM((parts, length, width), f32),
            pltpu.VMEM((parts - 1, length, width), f32),
            pltpu.VMEM((2, 2 * parts, width), f32),
            pltpu.VMEM((2, 2 * parts, width), f32),
            pltpu.VMEM((2, 2 * parts, width), f32),
            pltpu.VMEM((2, 2 * parts, width), f32),
            pltpu.VMEM((2, parts * length, LANES), f32),
            pltpu.VMEM((2, segs - 1, parts * length, LANES), f32),
            dma((2,)), dma((2, 2)), dma((2, 2)), dma((2, segs - 1)), dma((2, segs - 1)),
        ],
        compiler_params=pltpu.CompilerParams(collective_id=0, has_side_effects=True),
    )(state, metric, block_map, links.transpose(1, 2, 0))
    return result.reshape(state.shape)


def solution(mesh):
    in_specs = (P(("seg", "blk"), None, None, None), P(("seg", "blk"), None, None, None), P(), P())
    out_specs = P(("seg", "blk"), None, None, None)
    return jax.shard_map(
        on_device, mesh=mesh, in_specs=in_specs, out_specs=out_specs, check_vma=False
    )
```
